256 devices in a mesh: dp: 2 (over core), tm: 32 (over z, y), space: 4 (over x).
Axes of the slice: x: 4, y: 4, z: 8, core: 2. Of those that a mesh axis runs over, the one named last changes fastest.
Arguments:
- latents: bfloat16 [2, 64, 8, 80, 512], P('dp', 'tm', 'space'), may hold values from -6 to 6
- norm_gain: float32 [512], replicated, may hold values from 0.25 to 1.75
- kernel: bfloat16 [13824, 512], P(None, 'dp'), may hold values from -0.0546875 to 0.0546875
- conv_bias: float32 [512], replicated, may hold values from -3 to 3
- out_grad: bfloat16 [2, 64, 8, 80, 512], P('dp', 'tm', 'space'), may hold values from -6 to 6
Outputs:
- block_out: bfloat16 [2, 64, 8, 80, 512], P('dp', 'tm', 'space')
- latent_grad: bfloat16 [2, 64, 8, 80, 512], P('dp', 'tm', 'space')
- kernel_grad: float32 [13824, 512], P('tm', 'dp')
- gain_grad: float32 [512], replicated
- bias_grad: float32 [512], replicated
The draws below stay inside these ranges and needn't reach their ends.
All inputs are finite; a program needn't handle non-finite values.
Results may differ from the reference program's by a relative error of at most 0.0029.
Values may be sent and summed in bfloat16 or wider, within the bound.
No kernel may reach another device: no remote copies, remote signals or barrier semaphores. Data moves between devices by JAX's collectives and lax.ppermute only.
A program may use at most 128 MiB of HBM per device.

```python
import jax
import jax.numpy as jnp
from jax import lax

C = 512
TAPS = 27
W = 80
CLIPS = 2
FRAMES = 64
H = 8


def block_levels(stream_key, shape, split, least, high):
    level = 1.0
    for dim, shards_of in split:
        heights = jax.random.uniform(jax.random.fold_in(jax.random.fold_in(stream_key, 6), dim), (shards_of,), jnp.float32, least / len(split), high / len(split))
        level = level * jnp.repeat(jnp.exp(heights), shape[dim] // shards_of).reshape((-1,) + (1,) * (len(shape) - 1 - dim))
    return level


def centred(own_key, shape, width, limit, shards=(), held_as=jnp.bfloat16):
    entries = width * jax.random.normal(own_key, shape, jnp.float32)
    if shards:
        entries = entries * block_levels(own_key, shape, shards, -0.22, 0.18)
    return jnp.clip(entries, -limit, limit).astype(held_as)


def setup_inputs(seed: int = 0) -> dict:
    keys = jax.random.split(jax.random.key(seed), 6)
    return {
        "latents": centred(keys[0], (CLIPS, FRAMES, H, W, C), 1.0, 6.0, ((0, 2), (1, 32), (2, 4))),
        "norm_gain": jnp.clip(1.0 + 0.15 * jax.random.normal(keys[1], (C,), jnp.float32), 0.25, 1.75),
        "kernel": centred(keys[2], (TAPS * C, C), (TAPS * C) ** -0.5, 0.0546875, ((1, 2),)),
        "conv_bias": centred(keys[3], (C,), 0.5, 3.0, (), jnp.float32),
        "out_grad": centred(keys[4], (CLIPS, FRAMES, H, W, C), 1.0, 6.0, ((0, 2), (1, 32), (2, 4))),
    }


def reference(latents, norm_gain, kernel, conv_bias, out_grad):
    chans = latents.shape[-1]
    floats = latents.astype(jnp.float32)
    scale = 1.0 / jnp.sqrt(lax.optimization_barrier(jnp.mean(floats * floats, axis=-1, keepdims=True)) + 1e-06)
    normed = floats * scale
    pre_act = normed * norm_gain
    act = jax.nn.silu(pre_act).astype(jnp.bfloat16)
    blocks = kernel.reshape(3, 3, 3, chans, chans)
    clip_count, frame_count, row_count, col_count = latents.shape[:4]
    grad_scale = 1.0 / jnp.sqrt(jnp.float32(clip_count * frame_count * row_count * col_count))
    padded = jnp.pad(act, ((0, 0), (2, 0), (1, 1), (1, 1), (0, 0)))
    grad_pad = jnp.pad(out_grad, ((0, 0), (0, 2), (1, 1), (1, 1), (0, 0)))
    grad_flat = out_grad.reshape(-1, chans)
    conv = jnp.zeros(latents.shape, jnp.float32)
    act_grad = jnp.zeros(latents.shape, jnp.float32)
    kernel_rows = []
    for tap_t in range(3):
        for tap_h in range(3):
            for tap_w in range(3):
                window = padded[:, tap_t:tap_t + frame_count, tap_h:tap_h + row_count, tap_w:tap_w + col_count, :]
                window = window.reshape(-1, chans)
                conv = conv + jnp.dot(window, blocks[tap_t, tap_h, tap_w], preferred_element_type=jnp.float32).reshape(latents.shape)
                kernel_rows.append(jnp.dot(window.T, grad_flat, preferred_element_type=jnp.float32))
                back = grad_pad[:, 2 - tap_t:2 - tap_t + frame_count, 2 - tap_h:2 - tap_h + row_count, 2 - tap_w:2 - tap_w + col_count, :]
                act_grad = act_grad + jnp.dot(back.reshape(-1, chans), blocks[tap_t, tap_h, tap_w].T, preferred_element_type=jnp.float32).reshape(latents.shape)
    block_out = (floats + conv + conv_bias).astype(jnp.bfloat16)
    kernel_grad = jnp.concatenate(kernel_rows, axis=0) * grad_scale
    grads = out_grad.astype(jnp.float32)
    bias_grad = lax.optimization_barrier(jnp.sum(grads.reshape(-1, chans), axis=0)) * grad_scale
    sig = jax.nn.sigmoid(pre_act)
    pre_grad = act_grad * sig * (1.0 + pre_act * (1.0 - sig))
    gain_grad = lax.optimization_barrier(jnp.sum((pre_grad * normed).reshape(-1, chans), axis=0)) * grad_scale
    normed_grad = pre_grad * norm_gain
    latent_grad = grads + scale * (normed_grad - normed * lax.optimization_barrier(jnp.mean(normed_grad * normed, axis=-1, keepdims=True)))
    return (block_out, latent_grad.astype(jnp.bfloat16), kernel_grad, gain_grad, bias_grad)
```

```python
import jax
import jax.numpy as jnp
from jax import lax
from jax.experimental import pallas as pl
from jax.experimental.pallas import tpu as pltpu
from jax.sharding import Mesh, PartitionSpec as P

F32 = jnp.float32
BF16 = jnp.bfloat16
COLS = 80
CH = 512
HALF = 256
CELLS = 320
TOTAL = 81920
EPS = 1e-06
BIG = pltpu.CompilerParams(vmem_limit_bytes=58 * 1024 * 1024)
AXES = {"dp": 2, "z": 8, "y": 4, "x": 4}


def class_of(block, k):
    return jnp.concatenate(
        [block[:, 64 * k : 64 * k + 64], block[:, HALF + 64 * k : HALF + 64 * k + 64]], axis=-1
    )


def normalised(floats):
    scale = 1.0 / jnp.sqrt(jnp.mean(floats * floats, axis=-1, keepdims=True) + EPS)
    return scale, floats * scale


def act_kernel(lat_ref, gain_ref, grad_ref, act_ref, mix_ref):
    for j in range(4):
        rows = pl.ds(COLS * j, COLS)
        floats = lat_ref[rows, :].astype(F32)
        _, normed = normalised(floats)
        pre_act = normed * gain_ref[...]
        act = pre_act / (1.0 + jnp.exp(-pre_act))
        act_ref[rows, :] = act.astype(BF16)
        grad = grad_ref[rows, :].astype(F32)
        for k in range(4):
            act_piece = class_of(act, k).astype(BF16)
            grad_piece = class_of(grad, k).astype(BF16)
            for other in range(4):
                mix_ref[4 * other + k, 0, rows, :] = act_piece
                mix_ref[4 * k + other, 1, rows, :] = grad_piece


def shifted_columns(block):
    wide = block.astype(F32)
    column = lax.broadcasted_iota(jnp.int32, wide.shape, 0)
    before = jnp.where(column == 0, 0.0, pltpu.roll(wide, 1, 0)).astype(BF16)
    after = jnp.where(column == COLS - 1, 0.0, pltpu.roll(wide, COLS - 1, 0)).astype(BF16)
    return before, block, after


def conv_kernel(
    lat_ref, bias_ref, act_ref, prev_ref, low_ref, high_ref, own_ref, oth_ref, out_ref, ext, acc
):
    step = pl.program_id(0)

    @pl.when(step == 0)
    def _():
        for f in range(4):
            for r in range(4):
                if r == 0:
                    block = low_ref[f]
                elif r == 3:
                    block = high_ref[f]
                elif f < 2:
                    block = prev_ref[f, r - 1]
                else:
                    block = act_ref[f - 2, r - 1]
                for s, shifted in enumerate(shifted_columns(block)):
                    ext[s, f, r] = shifted
        acc[...] = jnp.zeros_like(acc)

    tap_t, tap_h = step // 3, step % 3
    window = jnp.concatenate(
        [ext[c, pl.ds(tap_t, 2), pl.ds(tap_h, 2)].reshape(CELLS, CH) for c in range(3)], axis=-1
    )
    acc[0] += jnp.dot(window, own_ref[...], preferred_element_type=F32)
    acc[1] += jnp.dot(window, oth_ref[...], preferred_element_type=F32)

    @pl.when(step == 8)
    def _():
        me = lax.axis_index("dp")
        for half in range(2):
            first = half * HALF
            chans = pl.ds(first, HALF)
            conv = jnp.where(me == half, acc[0], acc[1])
            out_ref[:, chans] = (
                lat_ref[:, chans].astype(F32) + conv + bias_ref[:, chans]
            ).astype(BF16)


def back_kernel(
    lat_ref,
    gain_ref,
    grad_ref,
    next_ref,
    low_ref,
    high_ref,
    own_ref,
    oth_ref,
    out_ref,
    sums_ref,
    ext,
    acc,
):
    step = pl.program_id(0)

    @pl.when(step == 0)
    def _():
        me = lax.axis_index("dp")
        for f in range(4):
            for r in range(4):
                if r == 0:
                    block = low_ref[f]
                elif r == 3:
                    block = high_ref[f]
                elif f < 2:
                    block = grad_ref[f, r - 1]
                else:
                    block = next_ref[f - 2, r - 1]
                for s, shifted in enumerate(shifted_columns(block)):
                    first, second = shifted[:, :HALF], shifted[:, HALF:]
                    ext[0, s, f, r] = jnp.where(me == 0, first, second)
                    ext[1, s, f, r] = jnp.where(me == 0, second, first)
        acc[...] = jnp.zeros_like(acc)

    tap_t, tap_h = step // 3, step % 3
    windows = []
    weights = []
    for half, ref in enumerate((own_ref, oth_ref)):
        for c in range(3):
            windows.append(
                ext[half, 2 - c, pl.ds(2 - tap_t, 2), pl.ds(2 - tap_h, 2)].reshape(CELLS, HALF)
            )
            weights.append(ref[pl.ds(CH * c, CH), :])
    acc[...] += lax.dot_general(
        jnp.concatenate(windows, axis=-1),
        jnp.concatenate(weights, axis=-1),
        (((1,), (1,)), ((), ())),
        preferred_element_type=F32,
    )

    @pl.when(step == 8)
    def _():
        gain_sum = jnp.zeros((1, CH), F32)
        bias_sum = jnp.zeros((1, CH), F32)
        gain = gain_ref[...]
        for j in range(4):
            rows = pl.ds(COLS * j, COLS)
            floats = lat_ref[rows, :].astype(F32)
            scale, normed = normalised(floats)
            pre_act = normed * gain
            sig = 1.0 / (1.0 + jnp.exp(-pre_act))
            pre_grad = acc[rows, :] * sig * (1.0 + pre_act * (1.0 - sig))
            grads = grad_ref[j // 2, j % 2].astype(F32)
            gain_sum += jnp.sum(pre_grad * normed, axis=0, keepdims=True)
            bias_sum += jnp.sum(grads, axis=0, keepdims=True)
            normed_grad = pre_grad * gain
            along = jnp.mean(normed_grad * normed, axis=-1, keepdims=True)
            out_ref[rows, :] = (grads + scale * (normed_grad - normed * along)).astype(BF16)
        for part in range(4):
            sums_ref[pl.ds(part, 1), :] = gain_sum[:, 128 * part : 128 * part + 128]
            sums_ref[pl.ds(4 + part, 1), :] = bias_sum[:, 128 * part : 128 * part + 128]


def weight_kernel(mix_ref, halo_ref, sums_ref, keep_ref, send_ref, acts, grads, acc):
    grad_scale = 1.0 / (TOTAL**0.5)
    zero = jnp.zeros((10, COLS, 128), BF16)
    grads[:, pl.ds(0, 1)] = zero.reshape(10, 1, COLS, 128)
    grads[:, pl.ds(9, 1)] = zero.reshape(10, 1, COLS, 128)
    for y in range(4):
        for x in range(4):
            for f in range(2):
                for r in range(2):
                    row = 2 * x + r
                    grads[2 * y + f, 1 + row] = mix_ref[4 * y + x, 1, f, r]
                    block = mix_ref[4 * y + x, 0, f, r]
                    for c, shifted in enumerate(shifted_columns(block)):
                        acts[y, c, pl.ds(640 * f + COLS * row, COLS), :] = shifted
    for x in range(4):
        for f in range(2):
            for r in range(2):
                grads[8 + f, 1 + 2 * x + r] = halo_ref[x, f, r]
    acc[...] = jnp.zeros_like(acc)

    @pl.loop(0, 4)
    def _(pair):
        left = jnp.concatenate([acts[pair, c] for c in range(3)], axis=-1)
        right = jnp.concatenate(
            [
                grads[pl.ds(2 * pair + 2 - a, 2), pl.ds(2 - b, 8)].reshape(1280, 128)
                for a in range(3)
                for b in range(3)
            ],
            axis=-1,
        )
        acc[...] += lax.dot_general(
            left, right, (((0,), (0,)), ((), ())), preferred_element_type=F32
        )

    me = lax.axis_index("dp")
    for ab in range(9):
        for c in range(3):
            block = acc[pl.ds(128 * c, 128), pl.ds(128 * ab, 128)] * grad_scale
            top, bottom = block[:64], block[64:]
            first = jnp.concatenate([top[:, :64], bottom[:, :64]], axis=-1)
            second = jnp.concatenate([top[:, 64:], bottom[:, 64:]], axis=-1)
            rows = pl.ds(64 * (3 * ab + c), 64)
            keep_ref[rows, :] = jnp.where(me == 0, first, second)
            send_ref[rows, :] = jnp.where(me == 0, second, first)
    keep_ref[pl.ds(1728, 8), :] = sums_ref[...] * grad_scale
    send_ref[pl.ds(1728, 8), :] = sums_ref[...] * grad_scale


def first_tap(z, x):
    return jnp.minimum(lax.div(lax.div(27 * z - x + 3, 4), 2), 23)


def split_kernel(keep_ref, got_ref, piece_ref, mine_ref, both):
    both[...] = keep_ref[...] + got_ref[...]
    z, x = lax.axis_index("z"), lax.axis_index("x")
    total = both[pl.ds(1728, 8), :]
    high = total.astype(BF16).astype(F32)
    mid = (total - high).astype(BF16).astype(F32)
    low = total - high - mid
    terms = jnp.concatenate([high, mid, low, jnp.zeros_like(low)], axis=0).astype(BF16)
    for k in range(8):
        target = lax.rem(z + k, 8)
        start = pl.multiple_of(64 * first_tap(target, x), 64)
        if k == 0:
            mine_ref[pl.ds(0, 256), :] = both[pl.ds(start, 256), :]
            mine_ref[pl.ds(256, 8), :] = total
        else:
            piece_ref[k - 1, pl.ds(0, 256), :] = both[pl.ds(start, 256), :].astype(BF16)
            piece_ref[k - 1, pl.ds(256, 32), :] = terms


def sum_kernel(mine_ref, *refs):
    got_refs, out_ref, taps = refs[:7], refs[7], refs[8]
    z, x = lax.axis_index("z"), lax.axis_index("x")
    block = mine_ref[pl.ds(0, 256), :]
    total = mine_ref[pl.ds(256, 8), :]
    for got in got_refs:
        block += got[pl.ds(0, 256), :].astype(F32)
        terms = got[pl.ds(256, 32), :].astype(F32)
        total += terms[0:8] + terms[8:16] + terms[16:24]
    taps[...] = block
    lane = lax.broadcasted_iota(jnp.int32, (64, 128), 1)
    for y in range(4):
        group = lax.div(27 * (4 * z + y), 4)
        unit = lax.div(group - x + 3, 4)
        tap = lax.div(unit, 2) - first_tap(z, x)
        odd = lax.rem(unit, 2)
        here = taps[pl.ds(pl.multiple_of(64 * jnp.minimum(tap, 3), 64), 64), :]
        after = taps[pl.ds(pl.multiple_of(64 * jnp.minimum(tap + 1, 3), 64), 64), :]
        crossed = pltpu.roll(jnp.where(lane >= 64, here, after), 64, 1)
        piece = jnp.where(odd == 1, crossed, here)
        for other in range(4):
            out_ref[4 * y + other, pl.ds(0, 64), :] = piece
            out_ref[4 * y + other, pl.ds(64, 8), :] = total


def final_kernel(got_ref, out_ref, sums_ref, rows):
    z, y = lax.axis_index("z"), lax.axis_index("y")
    index = 4 * z + y
    group = lax.div(27 * index, 4)
    for j in range(8):
        source = lax.rem(group + j, 4)
        pieces = []
        for part in range(4):
            block = got_ref[4 * part + source, pl.ds(0, 64), :]
            pieces.append(block[:, :64] if j < 4 else block[:, 64:])
        rows[pl.ds(64 * j, 64), :] = jnp.concatenate(pieces, axis=-1)
    offset = pl.multiple_of(16 * lax.rem(27 * index, 4), 16)
    out_ref[...] = rows[pl.ds(offset, 432), :]
    total = got_ref[0, pl.ds(64, 8), :]
    for k in range(1, 16):
        total += got_ref[k, pl.ds(64, 8), :]
    sums_ref[...] = total


def shape(dims, dtype):
    return jax.ShapeDtypeStruct(dims, dtype)


def moved(block, axis, distance):
    count = AXES[axis]
    return lax.ppermute(block, axis, [(i, (i + distance) % count) for i in range(count)])


def neighbour(block, axes, count, distance):
    route = [(i, i + distance) for i in range(count) if 0 <= i + distance < count]
    return lax.ppermute(block, axes, route)


def whole(dims):
    return pl.BlockSpec(dims, lambda i: (0,) * len(dims))


def on_device(latents, norm_gain, kernel, conv_bias, out_grad):
    lat_flat = latents.reshape(CELLS, CH)
    gain_row = norm_gain.reshape(1, CH)
    bias_row = conv_bias.reshape(1, CH)
    grad = out_grad.reshape(2, 2, COLS, CH)

    kernel_other = moved(kernel, "dp", 1)
    later = neighbour(grad, ("z", "y"), 32, -1)

    act_flat, mix = pl.pallas_call(
        act_kernel,
        out_shape=(shape((CELLS, CH), BF16), shape((16, 2, CELLS, 128), BF16)),
        compiler_params=BIG,
        name="act",
    )(lat_flat, gain_row, grad.reshape(CELLS, CH))
    act = act_flat.reshape(2, 2, COLS, CH)
    earlier = neighbour(act, ("z", "y"), 32, 1)

    mixed = lax.all_to_all(mix, ("y", "x"), 0, 0).reshape(16, 2, 2, 2, COLS, 128)
    halo = neighbour(mixed[0:4, 1], "z", 8, -1)

    frames_grad = jnp.concatenate([grad, later], axis=0)
    frames_act = jnp.concatenate([earlier, act], axis=0)
    edge_up = jnp.stack([frames_grad[:, 1], frames_act[:, 1]])
    edge_down = jnp.stack([frames_grad[:, 0], frames_act[:, 0]])
    low = neighbour(edge_up, "x", 4, 1)
    high = neighbour(edge_down, "x", 4, -1)

    weight_specs = [pl.BlockSpec((3 * CH, HALF), lambda i: (i, 0))] * 2
    tile = (2, 2, COLS, CH)
    edge = (4, COLS, CH)
    latent_grad, sums = pl.pallas_call(
        back_kernel,
        grid=(9,),
        in_specs=[whole((CELLS, CH)), whole((1, CH)), whole(tile), whole(tile)]
        + [whole(edge), whole(edge)]
        + weight_specs,
        out_specs=(whole((CELLS, CH)), whole((8, 128))),
        out_shape=(shape((CELLS, CH), BF16), shape((8, 128), F32)),
        scratch_shapes=[
            pltpu.VMEM((2, 3, 4, 4, COLS, HALF), BF16),
            pltpu.VMEM((CELLS, CH), F32),
        ],
        compiler_params=BIG,
        cost_estimate=pl.CostEstimate(
            flops=2 * CELLS * 27 * CH * CH, bytes_accessed=16_000_000, transcendentals=0
        ),
        name="back",
    )(lat_flat, gain_row, grad, later, low[0], high[0], kernel, kernel_other)

    block_out = pl.pallas_call(
        conv_kernel,
        grid=(9,),
        in_specs=[whole((CELLS, CH)), whole((1, CH)), whole(tile), whole(tile)]
        + [whole(edge), whole(edge)]
        + weight_specs,
        out_specs=whole((CELLS, CH)),
        out_shape=shape((CELLS, CH), BF16),
        scratch_shapes=[
            pltpu.VMEM((3, 4, 4, COLS, CH), BF16),
            pltpu.VMEM((2, CELLS, HALF), F32),
        ],
        compiler_params=BIG,
        cost_estimate=pl.CostEstimate(
            flops=2 * CELLS * 27 * CH * CH, bytes_accessed=16_000_000, transcendentals=0
        ),
        name="conv",
    )(lat_flat, bias_row, act, earlier, low[1], high[1], kernel, kernel_other)

    keep, send = pl.pallas_call(
        weight_kernel,
        out_shape=(shape((1736, 128), F32), shape((1736, 128), F32)),
        scratch_shapes=[
            pltpu.VMEM((4, 3, 1280, 128), BF16),
            pltpu.VMEM((10, 10, COLS, 128), BF16),
            pltpu.VMEM((384, 1152), F32),
        ],
        compiler_params=BIG,
        cost_estimate=pl.CostEstimate(
            flops=2 * CELLS * 27 * CH * CH, bytes_accessed=5_000_000, transcendentals=0
        ),
        name="weight",
    )(mixed, halo, sums)
    got = moved(send, "dp", 1)

    pieces, mine = pl.pallas_call(
        split_kernel,
        out_shape=(shape((7, 288, 128), BF16), shape((264, 128), F32)),
        scratch_shapes=[pltpu.VMEM((1736, 128), F32)],
        compiler_params=BIG,
        name="split",
    )(keep, got)
    arrived = [moved(pieces[k - 1], "z", k) for k in range(1, 8)]
    spread = pl.pallas_call(
        sum_kernel,
        out_shape=shape((16, 72, 128), F32),
        scratch_shapes=[pltpu.VMEM((256, 128), F32)],
        compiler_params=BIG,
        name="sum",
    )(mine, *arrived)
    gathered = lax.all_to_all(spread, ("y", "x"), 0, 0)
    kernel_grad, totals = pl.pallas_call(
        final_kernel,
        out_shape=(shape((432, 256), F32), shape((8, 128), F32)),
        scratch_shapes=[pltpu.VMEM((512, 256), F32)],
        compiler_params=BIG,
        name="final",
    )(gathered)
    return (
        block_out.reshape(latents.shape),
        latent_grad.reshape(latents.shape),
        kernel_grad,
        totals[:4].reshape(CH),
        totals[4:].reshape(CH),
    )


def solution(mesh):
    fine = Mesh(mesh.devices.reshape(2, 8, 4, 4), ("dp", "z", "y", "x"))
    cells = P("dp", ("z", "y"), "x", None, None)
    return jax.shard_map(
        on_device,
        mesh=fine,
        in_specs=(cells, P(), P(None, "dp"), P(), cells),
        out_specs=(cells, cells, P(("z", "y"), "dp"), P(), P()),
        check_vma=False,
    )
```

```python
import jax
import jax.numpy as jnp
from jax import lax
from jax.experimental import pallas as pl
from jax.experimental.pallas import tpu as pltpu
from jax.sharding import Mesh, PartitionSpec as P

F32 = jnp.float32
BF16 = jnp.bfloat16
COLS = 80
CH = 512
HALF = 256
CELLS = 320
TOTAL = 81920
EPS = 1e-06
BIG = pltpu.CompilerParams(vmem_limit_bytes=58 * 1024 * 1024)
AXES = {"dp": 2, "z": 8, "y": 4, "x": 4}


def class_of(block, k):
    return jnp.concatenate(
        [block[:, 64 * k : 64 * k + 64], block[:, HALF + 64 * k : HALF + 64 * k + 64]], axis=-1
    )


def normalised(floats):
    scale = 1.0 / jnp.sqrt(jnp.mean(floats * floats, axis=-1, keepdims=True) + EPS)
    return scale, floats * scale


def spread_kernel(grad_ref, mix_ref):
    for j in range(4):
        rows = pl.ds(COLS * j, COLS)
        grad = grad_ref[rows, :].astype(F32)
        for k in range(4):
            piece = class_of(grad, k).astype(BF16)
            for other in range(4):
                mix_ref[4 * k + other, rows, :] = piece


def act_kernel(lat_ref, gain_ref, act_ref, mix_ref):
    for j in range(4):
        rows = pl.ds(COLS * j, COLS)
        floats = lat_ref[rows, :].astype(F32)
        _, normed = normalised(floats)
        pre_act = normed * gain_ref[...]
        act = pre_act / (1.0 + jnp.exp(-pre_act))
        act_ref[rows, :] = act.astype(BF16)
        for k in range(4):
            piece = class_of(act, k).astype(BF16)
            for other in range(4):
                mix_ref[4 * other + k, rows, :] = piece


def shifted_columns(block):
    wide = block.astype(F32)
    column = lax.broadcasted_iota(jnp.int32, wide.shape, 0)
    before = jnp.where(column == 0, 0.0, pltpu.roll(wide, 1, 0)).astype(BF16)
    after = jnp.where(column == COLS - 1, 0.0, pltpu.roll(wide, COLS - 1, 0)).astype(BF16)
    return before, block, after


def conv_kernel(
    lat_ref, bias_ref, act_ref, prev_ref, low_ref, high_ref, own_ref, oth_ref, out_ref, ext, acc
):
    step = pl.program_id(0)

    @pl.when(step == 0)
    def _():
        for f in range(4):
            for r in range(4):
                if r == 0:
                    block = low_ref[f]
                elif r == 3:
                    block = high_ref[f]
                elif f < 2:
                    block = prev_ref[f, r - 1]
                else:
                    block = act_ref[f - 2, r - 1]
                for s, shifted in enumerate(shifted_columns(block)):
                    ext[s, f, r] = shifted
        acc[...] = jnp.zeros_like(acc)

    tap_t, tap_h = step // 3, step % 3
    window = jnp.concatenate(
        [ext[c, pl.ds(tap_t, 2), pl.ds(tap_h, 2)].reshape(CELLS, CH) for c in range(3)], axis=-1
    )
    acc[0] += jnp.dot(window, own_ref[...], preferred_element_type=F32)
    acc[1] += jnp.dot(window, oth_ref[...], preferred_element_type=F32)

    @pl.when(step == 8)
    def _():
        me = lax.axis_index("dp")
        for half in range(2):
            first = half * HALF
            chans = pl.ds(first, HALF)
            conv = jnp.where(me == half, acc[0], acc[1])
            out_ref[:, chans] = (
                lat_ref[:, chans].astype(F32) + conv + bias_ref[:, chans]
            ).astype(BF16)


def back_kernel(
    lat_ref,
    gain_ref,
    grad_ref,
    next_ref,
    low_ref,
    high_ref,
    own_ref,
    oth_ref,
    out_ref,
    sums_ref,
    ext,
    acc,
):
    step = pl.program_id(0)

    @pl.when(step == 0)
    def _():
        me = lax.axis_index("dp")
        for f in range(4):
            for r in range(4):
                if r == 0:
                    block = low_ref[f]
                elif r == 3:
                    block = high_ref[f]
                elif f < 2:
                    block = grad_ref[f, r - 1]
                else:
                    block = next_ref[f - 2, r - 1]
                for s, shifted in enumerate(shifted_columns(block)):
                    first, second = shifted[:, :HALF], shifted[:, HALF:]
                    ext[0, s, f, r] = jnp.where(me == 0, first, second)
                    ext[1, s, f, r] = jnp.where(me == 0, second, first)
        acc[...] = jnp.zeros_like(acc)

    tap_t, tap_h = step // 3, step % 3
    windows = []
    weights = []
    for half, ref in enumerate((own_ref, oth_ref)):
        for c in range(3):
            windows.append(
                ext[half, 2 - c, pl.ds(2 - tap_t, 2), pl.ds(2 - tap_h, 2)].reshape(CELLS, HALF)
            )
            weights.append(ref[pl.ds(CH * c, CH), :])
    acc[...] += lax.dot_general(
        jnp.concatenate(windows, axis=-1),
        jnp.concatenate(weights, axis=-1),
        (((1,), (1,)), ((), ())),
        preferred_element_type=F32,
    )

    @pl.when(step == 8)
    def _():
        gain_sum = jnp.zeros((1, CH), F32)
        bias_sum = jnp.zeros((1, CH), F32)
        gain = gain_ref[...]
        for j in range(4):
            rows = pl.ds(COLS * j, COLS)
            floats = lat_ref[rows, :].astype(F32)
            scale, normed = normalised(floats)
            pre_act = normed * gain
            sig = 1.0 / (1.0 + jnp.exp(-pre_act))
            pre_grad = acc[rows, :] * sig * (1.0 + pre_act * (1.0 - sig))
            grads = grad_ref[j // 2, j % 2].astype(F32)
            gain_sum += jnp.sum(pre_grad * normed, axis=0, keepdims=True)
            bias_sum += jnp.sum(grads, axis=0, keepdims=True)
            normed_grad = pre_grad * gain
            along = jnp.mean(normed_grad * normed, axis=-1, keepdims=True)
            out_ref[rows, :] = (grads + scale * (normed_grad - normed * along)).astype(BF16)
        for part in range(4):
            sums_ref[pl.ds(part, 1), :] = gain_sum[:, 128 * part : 128 * part + 128]
            sums_ref[pl.ds(4 + part, 1), :] = bias_sum[:, 128 * part : 128 * part + 128]


def weight_kernel(act_ref, grad_ref, halo_ref, sums_ref, keep_ref, send_ref, acts, grads, acc):
    grad_scale = 1.0 / (TOTAL**0.5)
    zero = jnp.zeros((10, COLS, 128), BF16)
    grads[:, pl.ds(0, 1)] = zero.reshape(10, 1, COLS, 128)
    grads[:, pl.ds(9, 1)] = zero.reshape(10, 1, COLS, 128)
    for y in range(4):
        for x in range(4):
            for f in range(2):
                for r in range(2):
                    row = 2 * x + r
                    grads[2 * y + f, 1 + row] = grad_ref[4 * y + x, f, r]
                    block = act_ref[4 * y + x, f, r]
                    for c, shifted in enumerate(shifted_columns(block)):
                        acts[y, c, pl.ds(640 * f + COLS * row, COLS), :] = shifted
    for x in range(4):
        for f in range(2):
            for r in range(2):
                grads[8 + f, 1 + 2 * x + r] = halo_ref[x, f, r]
    acc[...] = jnp.zeros_like(acc)

    @pl.loop(0, 4)
    def _(pair):
        left = jnp.concatenate([acts[pair, c] for c in range(3)], axis=-1)
        right = jnp.concatenate(
            [
                grads[pl.ds(2 * pair + 2 - a, 2), pl.ds(2 - b, 8)].reshape(1280, 128)
                for a in range(3)
                for b in range(3)
            ],
            axis=-1,
        )
        acc[...] += lax.dot_general(
            left, right, (((0,), (0,)), ((), ())), preferred_element_type=F32
        )

    me = lax.axis_index("dp")
    for ab in range(9):
        for c in range(3):
            block = acc[pl.ds(128 * c, 128), pl.ds(128 * ab, 128)] * grad_scale
            top, bottom = block[:64], block[64:]
            first = jnp.concatenate([top[:, :64], bottom[:, :64]], axis=-1)
            second = jnp.concatenate([top[:, 64:], bottom[:, 64:]], axis=-1)
            rows = pl.ds(64 * (3 * ab + c), 64)
            keep_ref[rows, :] = jnp.where(me == 0, first, second)
            send_ref[rows, :] = jnp.where(me == 0, second, first)
    keep_ref[pl.ds(1728, 8), :] = sums_ref[...] * grad_scale
    send_ref[pl.ds(1728, 8), :] = sums_ref[...] * grad_scale


def first_unit(index, x):
    return lax.div(lax.div(27 * index, 4) - x + 3, 4)


def split_kernel(keep_ref, got_ref, piece_ref, both):
    both[pl.ds(0, 1736), :] = keep_ref[...] + got_ref[...]
    x = lax.axis_index("x")
    total = both[pl.ds(1728, 8), :]
    high = total.astype(BF16).astype(F32)
    terms = jnp.concatenate([high, total - high], axis=0).astype(BF16)
    lane = lax.broadcasted_iota(jnp.int32, (64, 128), 1)
    for index in range(32):
        unit = first_unit(index, x)
        row = pl.multiple_of(64 * lax.div(unit, 2), 64)
        here = both[pl.ds(row, 64), :]
        after = both[pl.ds(row + 64, 64), :]
        crossed = pltpu.roll(jnp.where(lane >= 64, here, after), 64, 1)
        piece = jnp.where(lax.rem(unit, 2) == 1, crossed, here)
        piece_ref[index, pl.ds(0, 64), :] = piece.astype(BF16)
        piece_ref[index, pl.ds(64, 16), :] = terms


def sum_kernel(got_ref, out_ref):
    total = jnp.zeros((8, 128), F32)
    parts = []
    for y in range(4):
        block = jnp.zeros((64, 128), F32)
        for z in range(8):
            block += got_ref[4 * z + y, pl.ds(0, 64), :].astype(F32)
            terms = got_ref[4 * z + y, pl.ds(64, 16), :].astype(F32)
            total += terms[0:8] + terms[8:16]
        parts.append(block)
    for unit in range(2):
        lanes = slice(64 * unit, 64 * unit + 64)
        out_ref[pl.ds(64 * unit, 64), :] = jnp.concatenate([p[:, lanes] for p in parts], axis=-1)
    out_ref[pl.ds(128, 8), :] = jnp.concatenate([total, total], axis=-1)


def final_kernel(own_ref, one_ref, two_ref, three_ref, out_ref, sums_ref, held, rows):
    z, y, x = lax.axis_index("z"), lax.axis_index("y"), lax.axis_index("x")
    index = 4 * z + y
    group = lax.div(27 * index, 4)
    total = jnp.zeros((8, 128), F32)
    for k, ref in enumerate((own_ref, one_ref, two_ref, three_ref)):
        held[lax.rem(x - k + 4, 4)] = ref[...]
    for k in range(4):
        total += held[k, pl.ds(128, 8), pl.ds(0, 128)]
    sums_ref[...] = total
    for j in range(8):
        source = lax.rem(group + j, 4)
        rows[pl.ds(64 * j, 64), :] = held[source, pl.ds(64 * (j // 4), 64), :]
    offset = pl.multiple_of(16 * lax.rem(27 * index, 4), 16)
    out_ref[...] = rows[pl.ds(offset, 432), :]


def shape(dims, dtype):
    return jax.ShapeDtypeStruct(dims, dtype)


def moved(block, axis, distance):
    count = AXES[axis]
    return lax.ppermute(block, axis, [(i, (i + distance) % count) for i in range(count)])


def neighbour(block, axes, count, distance):
    route = [(i, i + distance) for i in range(count) if 0 <= i + distance < count]
    return lax.ppermute(block, axes, route)


def whole(dims):
    return pl.BlockSpec(dims, lambda i: (0,) * len(dims))


def on_device(latents, norm_gain, kernel, conv_bias, out_grad):
    lat_flat = latents.reshape(CELLS, CH)
    gain_row = norm_gain.reshape(1, CH)
    bias_row = conv_bias.reshape(1, CH)
    grad = out_grad.reshape(2, 2, COLS, CH)

    kernel_other = moved(kernel, "dp", 1)
    later = neighbour(grad, ("z", "y"), 32, -1)
    grad_mix = pl.pallas_call(
        spread_kernel,
        out_shape=shape((16, CELLS, 128), BF16),
        compiler_params=BIG,
        name="spread",
    )(grad.reshape(CELLS, CH))
    grad_mix = lax.all_to_all(grad_mix, ("y", "x"), 0, 0).reshape(16, 2, 2, COLS, 128)
    act_flat, act_mix = pl.pallas_call(
        act_kernel,
        out_shape=(shape((CELLS, CH), BF16), shape((16, CELLS, 128), BF16)),
        compiler_params=BIG,
        name="act",
    )(lat_flat, gain_row)
    act = act_flat.reshape(2, 2, COLS, CH)
    act_mix = lax.all_to_all(act_mix, ("y", "x"), 0, 0).reshape(16, 2, 2, COLS, 128)
    halo = neighbour(grad_mix[0:4], "z", 8, -1)
    grad_low = neighbour(jnp.concatenate([grad[:, 1], later[:, 1]]), "x", 4, 1)
    grad_high = neighbour(jnp.concatenate([grad[:, 0], later[:, 0]]), "x", 4, -1)

    act_late, act_mix = lax.optimization_barrier((act, act_mix))
    earlier = neighbour(act_late, ("z", "y"), 32, 1)
    act_low = neighbour(jnp.concatenate([earlier[:, 1], act_late[:, 1]]), "x", 4, 1)
    act_high = neighbour(jnp.concatenate([earlier[:, 0], act_late[:, 0]]), "x", 4, -1)

    weight_specs = [pl.BlockSpec((3 * CH, HALF), lambda i: (i, 0))] * 2
    tile = (2, 2, COLS, CH)
    edge = (4, COLS, CH)
    latent_grad, sums = pl.pallas_call(
        back_kernel,
        grid=(9,),
        in_specs=[whole((CELLS, CH)), whole((1, CH)), whole(tile), whole(tile)]
        + [whole(edge), whole(edge)]
        + weight_specs,
        out_specs=(whole((CELLS, CH)), whole((8, 128))),
        out_shape=(shape((CELLS, CH), BF16), shape((8, 128), F32)),
        scratch_shapes=[
            pltpu.VMEM((2, 3, 4, 4, COLS, HALF), BF16),
            pltpu.VMEM((CELLS, CH), F32),
        ],
        compiler_params=BIG,
        cost_estimate=pl.CostEstimate(
            flops=2 * CELLS * 27 * CH * CH, bytes_accessed=16_000_000, transcendentals=0
        ),
        name="back",
    )(lat_flat, gain_row, grad, later, grad_low, grad_high, kernel, kernel_other)

    block_out = pl.pallas_call(
        conv_kernel,
        grid=(9,),
        in_specs=[whole((CELLS, CH)), whole((1, CH)), whole(tile), whole(tile)]
        + [whole(edge), whole(edge)]
        + weight_specs,
        out_specs=whole((CELLS, CH)),
        out_shape=shape((CELLS, CH), BF16),
        scratch_shapes=[
            pltpu.VMEM((3, 4, 4, COLS, CH), BF16),
            pltpu.VMEM((2, CELLS, HALF), F32),
        ],
        compiler_params=BIG,
        cost_estimate=pl.CostEstimate(
            flops=2 * CELLS * 27 * CH * CH, bytes_accessed=16_000_000, transcendentals=0
        ),
        name="conv",
    )(lat_flat, bias_row, act, earlier, act_low, act_high, kernel, kernel_other)

    keep, send = pl.pallas_call(
        weight_kernel,
        out_shape=(shape((1736, 128), F32), shape((1736, 128), F32)),
        scratch_shapes=[
            pltpu.VMEM((4, 3, 1280, 128), BF16),
            pltpu.VMEM((10, 10, COLS, 128), BF16),
            pltpu.VMEM((384, 1152), F32),
        ],
        compiler_params=BIG,
        cost_estimate=pl.CostEstimate(
            flops=2 * CELLS * 27 * CH * CH, bytes_accessed=5_000_000, transcendentals=0
        ),
        name="weight",
    )(act_mix, grad_mix, halo, sums)
    got = moved(send, "dp", 1)

    pieces = pl.pallas_call(
        split_kernel,
        out_shape=shape((32, 80, 128), BF16),
        scratch_shapes=[pltpu.VMEM((1792, 128), F32)],
        compiler_params=BIG,
        name="split",
    )(keep, got)
    pieces = lax.all_to_all(pieces, ("z", "y"), 0, 0)
    summed = pl.pallas_call(
        sum_kernel,
        out_shape=shape((136, 256), F32),
        compiler_params=BIG,
        name="sum",
    )(pieces)
    around = [moved(summed, "x", k) for k in range(1, 4)]
    kernel_grad, totals = pl.pallas_call(
        final_kernel,
        out_shape=(shape((432, 256), F32), shape((8, 128), F32)),
        scratch_shapes=[pltpu.VMEM((4, 136, 256), F32), pltpu.VMEM((512, 256), F32)],
        compiler_params=BIG,
        name="final",
    )(summed, *around)
    return (
        block_out.reshape(latents.shape),
        latent_grad.reshape(latents.shape),
        kernel_grad,
        totals[:4].reshape(CH),
        totals[4:].reshape(CH),
    )


def solution(mesh):
    fine = Mesh(mesh.devices.reshape(2, 8, 4, 4), ("dp", "z", "y", "x"))
    cells = P("dp", ("z", "y"), "x", None, None)
    return jax.shard_map(
        on_device,
        mesh=fine,
        in_specs=(cells, P(), P(None, "dp"), P(), cells),
        out_specs=(cells, cells, P(("z", "y"), "dp"), P(), P()),
        check_vma=False,
    )
```

```python
import jax
import jax.numpy as jnp
from jax import lax
from jax.experimental import pallas as pl
from jax.experimental.pallas import tpu as pltpu
from jax.sharding import Mesh, PartitionSpec as P


F32 = jnp.float32
BF16 = jnp.bfloat16
COLS = 80
CH = 512
HALF = 256
CELLS = 320
TOTAL = 81920
EPS = 1e-06


def room(mib):
    return pltpu.CompilerParams(vmem_limit_bytes=mib * 1024 * 1024)


AXES = {"dp": 2, "z": 8, "y": 4, "x": 4}


def class_of(block, k):
    return jnp.concatenate(
        [block[:, 64 * k : 64 * k + 64], block[:, HALF + 64 * k : HALF + 64 * k + 64]], axis=-1
    )


def normalised(floats):
    scale = 1.0 / jnp.sqrt(jnp.mean(floats * floats, axis=-1, keepdims=True) + EPS)
    return scale, floats * scale


def act_kernel(lat_ref, gain_ref, grad_ref, act_ref, mix_ref):
    for j in range(4):
        rows = pl.ds(COLS * j, COLS)
        floats = lat_ref[rows, :].astype(F32)
        _, normed = normalised(floats)
        pre_act = normed * gain_ref[...]
        act = pre_act / (1.0 + jnp.exp(-pre_act))
        act_ref[rows, :] = act.astype(BF16)
        grad = grad_ref[rows, :].astype(F32)
        for k in range(4):
            act_piece = class_of(act, k).astype(BF16)
            grad_piece = class_of(grad, k).astype(BF16)
            for other in range(4):
                mix_ref[4 * other + k, rows, :] = act_piece
                mix_ref[4 * k + other, pl.ds(CELLS + COLS * j, COLS), :] = grad_piece


def shifted_columns(block):
    wide = block.astype(F32)
    column = lax.broadcasted_iota(jnp.int32, wide.shape, 0)
    before = jnp.where(column == 0, 0.0, pltpu.roll(wide, 1, 0)).astype(BF16)
    after = jnp.where(column == COLS - 1, 0.0, pltpu.roll(wide, COLS - 1, 0)).astype(BF16)
    return before, block, after


def moved_columns(block, distance):
    column = lax.broadcasted_iota(jnp.int32, block.shape, 0)
    if distance == 1:
        return jnp.where(column == 0, 0.0, pltpu.roll(block, 1, 0))
    return jnp.where(column == COLS - 1, 0.0, pltpu.roll(block, COLS - 1, 0))


def conv_kernel(
    lat_ref, bias_ref, act_ref, prev_ref, low_ref, high_ref, own_ref, oth_ref, out_ref, ext, acc
):
    tap_t = pl.program_id(0)

    @pl.when(tap_t == 0)
    def _():
        for f in range(4):
            ext[f, 0] = low_ref[f]
            ext[f, 3] = high_ref[f]
            for r in range(2):
                ext[f, 1 + r] = prev_ref[2 * f + r] if f < 2 else act_ref[2 * f - 4 + r]
        acc[...] = jnp.zeros_like(acc)

    window = jnp.concatenate(
        [ext[pl.ds(tap_t, 2), b : b + 2].reshape(CELLS, CH) for b in range(3)], axis=-1
    )
    for c in range(3):
        for half, ref in enumerate((own_ref, oth_ref)):
            weights = jnp.concatenate(
                [ref[pl.ds(CH * (3 * b + c), CH), :] for b in range(3)], axis=0
            )
            acc[c, half] += jnp.dot(window, weights, preferred_element_type=F32)

    @pl.when(tap_t == 2)
    def _():
        me = lax.axis_index("dp")
        for half in range(2):
            chans = pl.ds(half * HALF, HALF)
            which = jnp.where(me == half, 0, 1)
            for j in range(4):
                rows = pl.ds(COLS * j, COLS)
                conv = (
                    moved_columns(acc[0, which, rows, :], 1)
                    + acc[1, which, rows, :]
                    + moved_columns(acc[2, which, rows, :], -1)
                )
                out_ref[rows, chans] = (
                    lat_ref[rows, chans].astype(F32) + conv + bias_ref[:, chans]
                ).astype(BF16)


def back_kernel(
    lat_ref,
    gain_ref,
    grad_ref,
    next_ref,
    low_ref,
    high_ref,
    own_ref,
    oth_ref,
    out_ref,
    sums_ref,
    ext,
    acc,
):
    tap_t = pl.program_id(0)

    @pl.when(tap_t == 0)
    def _():
        me = lax.axis_index("dp")
        for f in range(4):
            for r in range(4):
                if r == 0:
                    block = low_ref[f]
                elif r == 3:
                    block = high_ref[f]
                elif f < 2:
                    block = grad_ref[2 * f + r - 1]
                else:
                    block = next_ref[2 * f + r - 5]
                first, second = block[:, :HALF], block[:, HALF:]
                ext[f, r, :, pl.ds(0, HALF)] = jnp.where(me == 0, first, second)
                ext[f, r, :, pl.ds(HALF, HALF)] = jnp.where(me == 0, second, first)
        acc[...] = jnp.zeros_like(acc)

    window = jnp.concatenate(
        [ext[pl.ds(2 - tap_t, 2), 2 - b : 4 - b].reshape(CELLS, CH) for b in range(3)], axis=-1
    )
    for c in range(3):
        weights = []
        for b in range(3):
            taps = pl.ds(CH * (3 * b + c), CH)
            weights += [own_ref[taps, :], oth_ref[taps, :]]
        acc[c] += lax.dot_general(
            window,
            jnp.concatenate(weights, axis=-1),
            (((1,), (1,)), ((), ())),
            preferred_element_type=F32,
        )

    @pl.when(tap_t == 2)
    def _():
        gain_sum = jnp.zeros((1, CH), F32)
        bias_sum = jnp.zeros((1, CH), F32)
        gain = gain_ref[...]
        for j in range(4):
            rows = pl.ds(COLS * j, COLS)
            floats = lat_ref[rows, :].astype(F32)
            scale, normed = normalised(floats)
            pre_act = normed * gain
            sig = 1.0 / (1.0 + jnp.exp(-pre_act))
            act_grad = (
                moved_columns(acc[0, rows, :], -1)
                + acc[1, rows, :]
                + moved_columns(acc[2, rows, :], 1)
            )
            pre_grad = act_grad * sig * (1.0 + pre_act * (1.0 - sig))
            grads = grad_ref[j].astype(F32)
            gain_sum += jnp.sum(pre_grad * normed, axis=0, keepdims=True)
            bias_sum += jnp.sum(grads, axis=0, keepdims=True)
            normed_grad = pre_grad * gain
            along = jnp.mean(normed_grad * normed, axis=-1, keepdims=True)
            out_ref[rows, :] = (grads + scale * (normed_grad - normed * along)).astype(BF16)
        for part in range(4):
            sums_ref[pl.ds(part, 1), :] = gain_sum[:, 128 * part : 128 * part + 128]
            sums_ref[pl.ds(4 + part, 1), :] = bias_sum[:, 128 * part : 128 * part + 128]


def clear_edges(grads):
    frames = grads.shape[0]
    zero = jnp.zeros((frames, 1, COLS, 128), BF16)
    grads[:, pl.ds(0, 1)] = zero
    grads[:, pl.ds(9, 1)] = zero


def put_acts(mix_ref, y, acts, slot):
    for x in range(4):
        for f in range(2):
            for r in range(2):
                block = mix_ref[4 * y + x, 0, f, r]
                rows = pl.ds(640 * f + COLS * (2 * x + r), COLS)
                for c, shifted in enumerate(shifted_columns(block)):
                    acts[slot, c, rows, :] = shifted


def products(acts, grads, slot, frame):
    left = jnp.concatenate([acts[slot, c] for c in range(3)], axis=-1)
    right = jnp.concatenate(
        [
            grads[pl.ds(frame + 2 - a, 2), pl.ds(2 - b, 8)].reshape(1280, 128)
            for a in range(3)
            for b in range(3)
        ],
        axis=-1,
    )
    return lax.dot_general(left, right, (((0,), (0,)), ((), ())), preferred_element_type=F32)


def weight_kernel(mix_ref, acc_ref, acts, grads):
    clear_edges(grads)
    for y in range(4):
        if y < 3:
            put_acts(mix_ref, y, acts, y)
        for x in range(4):
            for f in range(2):
                for r in range(2):
                    grads[2 * y + f, 1 + 2 * x + r] = mix_ref[4 * y + x, 1, f, r]
    acc_ref[...] = jnp.zeros_like(acc_ref)

    @pl.loop(0, 3)
    def _(pair):
        acc_ref[...] += products(acts, grads, pair, 2 * pair)


def border_kernel(mix_ref, halo_ref, part_ref, sums_ref, keep_ref, send_ref, acts, grads, acc):
    grad_scale = 1.0 / (TOTAL**0.5)
    clear_edges(grads)
    put_acts(mix_ref, 3, acts, 0)
    for x in range(4):
        for f in range(2):
            for r in range(2):
                grads[f, 1 + 2 * x + r] = mix_ref[12 + x, 1, f, r]
                grads[2 + f, 1 + 2 * x + r] = halo_ref[x, f, r]
    acc[...] = part_ref[...] + products(acts, grads, 0, 0)
    me = lax.axis_index("dp")
    for ab in range(9):
        for c in range(3):
            block = acc[pl.ds(128 * c, 128), pl.ds(128 * ab, 128)] * grad_scale
            top, bottom = block[:64], block[64:]
            first = jnp.concatenate([top[:, :64], bottom[:, :64]], axis=-1)
            second = jnp.concatenate([top[:, 64:], bottom[:, 64:]], axis=-1)
            rows = pl.ds(64 * (3 * ab + c), 64)
            keep_ref[rows, :] = jnp.where(me == 0, first, second)
            send_ref[rows, :] = jnp.where(me == 0, second, first)
    keep_ref[pl.ds(1728, 8), :] = sums_ref[...] * grad_scale
    send_ref[pl.ds(1728, 8), :] = sums_ref[...] * grad_scale


def first_tap(z, x):
    return jnp.minimum(lax.div(lax.div(27 * z - x + 3, 4), 2), 23)


def split_kernel(keep_ref, got_ref, piece_ref, both):
    both[...] = keep_ref[...] + got_ref[...]
    x = lax.axis_index("x")
    total = both[pl.ds(1728, 8), :]
    high = total.astype(BF16).astype(F32)
    terms = jnp.concatenate([high, total - high], axis=0).astype(BF16)
    for z in range(8):
        start = pl.multiple_of(64 * first_tap(z, x), 64)
        piece_ref[z, pl.ds(0, 256), :] = both[pl.ds(start, 256), :].astype(BF16)
        piece_ref[z, pl.ds(256, 16), :] = terms


def sum_kernel(got_ref, out_ref, taps):
    z, x = lax.axis_index("z"), lax.axis_index("x")
    block = got_ref[0, pl.ds(0, 256), :].astype(F32)
    terms = got_ref[0, pl.ds(256, 16), :].astype(F32)
    for k in range(1, 8):
        block += got_ref[k, pl.ds(0, 256), :].astype(F32)
        terms += got_ref[k, pl.ds(256, 16), :].astype(F32)
    total = terms[:8] + terms[8:]
    taps[...] = block
    lane = lax.broadcasted_iota(jnp.int32, (64, 128), 1)
    for y in range(4):
        group = lax.div(27 * (4 * z + y), 4)
        unit = lax.div(group - x + 3, 4)
        tap = lax.div(unit, 2) - first_tap(z, x)
        here = taps[pl.ds(pl.multiple_of(64 * jnp.minimum(tap, 3), 64), 64), :]
        after = taps[pl.ds(pl.multiple_of(64 * jnp.minimum(tap + 1, 3), 64), 64), :]
        crossed = pltpu.roll(jnp.where(lane >= 64, here, after), 64, 1)
        piece = jnp.where(lax.rem(unit, 2) == 1, crossed, here)
        for other in range(4):
            out_ref[4 * y + other, pl.ds(0, 64), :] = piece
            out_ref[4 * y + other, pl.ds(64, 8), :] = total


def final_kernel(got_ref, out_ref, gain_out, bias_out, rows):
    z, y = lax.axis_index("z"), lax.axis_index("y")
    index = 4 * z + y
    group = lax.div(27 * index, 4)
    total = got_ref[0, pl.ds(64, 8), :]
    for k in range(1, 16):
        total += got_ref[k, pl.ds(64, 8), :]
    for part in range(4):
        lanes = pl.ds(128 * part, 128)
        gain_out[:, lanes] = total[part : part + 1]
        bias_out[:, lanes] = total[4 + part : 5 + part]
    for j in range(8):
        source = lax.rem(group + j, 4)
        pieces = []
        for part in range(4):
            block = got_ref[4 * part + source, pl.ds(0, 64), :]
            pieces.append(block[:, :64] if j < 4 else block[:, 64:])
        rows[pl.ds(64 * j, 64), :] = jnp.concatenate(pieces, axis=-1)
    offset = pl.multiple_of(16 * lax.rem(27 * index, 4), 16)
    out_ref[...] = rows[pl.ds(offset, 432), :]


def shape(dims, dtype):
    return jax.ShapeDtypeStruct(dims, dtype)


def moved(block, axis, distance):
    count = AXES[axis]
    return lax.ppermute(block, axis, [(i, (i + distance) % count) for i in range(count)])


def neighbour(block, axes, count, distance):
    route = [(i, i + distance) for i in range(count) if 0 <= i + distance < count]
    return lax.ppermute(block, axes, route)


def whole(dims):
    return pl.BlockSpec(dims, lambda i: (0,) * len(dims))


def on_device(latents, norm_gain, kernel, conv_bias, out_grad):
    lat_flat = latents.reshape(CELLS, CH)
    gain_row = norm_gain.reshape(1, CH)
    bias_row = conv_bias.reshape(1, CH)
    grad = out_grad.reshape(4, COLS, CH)

    kernel_other = moved(kernel, "dp", 1)
    later = neighbour(grad, ("z", "y"), 32, -1)
    up = jnp.stack([grad[1], grad[3], later[1], later[3]])
    down = jnp.stack([grad[0], grad[2], later[0], later[2]])
    grad_low = neighbour(up, "x", 4, 1)
    grad_high = neighbour(down, "x", 4, -1)
    act_flat, mix = pl.pallas_call(
        act_kernel,
        out_shape=(shape((CELLS, CH), BF16), shape((16, 2 * CELLS, 128), BF16)),
        compiler_params=room(58),
        name="act",
    )(lat_flat, gain_row, grad.reshape(CELLS, CH))
    mixed = lax.all_to_all(mix, ("y", "x"), 0, 0)

    weight_specs = [pl.BlockSpec((9 * CH, HALF), lambda i: (i, 0))] * 2
    tile, flat = whole((4, COLS, CH)), whole((CELLS, CH))
    estimate = pl.CostEstimate(
        flops=2 * CELLS * 27 * CH * CH, bytes_accessed=16_000_000, transcendentals=0
    )
    latent_grad, sums = pl.pallas_call(
        back_kernel,
        grid=(3,),
        in_specs=[flat, whole((1, CH)), tile, tile, tile, tile] + weight_specs,
        out_specs=(flat, whole((8, 128))),
        out_shape=(shape((CELLS, CH), BF16), shape((8, 128), F32)),
        scratch_shapes=[
            pltpu.VMEM((4, 4, COLS, CH), BF16),
            pltpu.VMEM((3, CELLS, CH), F32),
        ],
        compiler_params=room(52),
        cost_estimate=estimate,
        name="back",
    )(
        lat_flat,
        gain_row,
        grad,
        later,
        grad_low,
        grad_high,
        kernel,
        kernel_other,
    )

    act_late, mixed = lax.optimization_barrier((act_flat.reshape(4, COLS, CH), mixed))
    border = lax.slice(mixed, (0, CELLS, 0), (4, 2 * CELLS, 128))
    halo = neighbour(border, "z", 8, -1).reshape(4, 2, 2, COLS, 128)
    mixed = mixed.reshape(16, 2, 2, 2, COLS, 128)
    earlier = neighbour(act_late, ("z", "y"), 32, 1)
    act_up = jnp.stack([earlier[1], earlier[3], act_late[1], act_late[3]])
    act_down = jnp.stack([earlier[0], earlier[2], act_late[0], act_late[2]])
    act_low = neighbour(act_up, "x", 4, 1)
    act_high = neighbour(act_down, "x", 4, -1)
    block_out = pl.pallas_call(
        conv_kernel,
        grid=(3,),
        in_specs=[flat, whole((1, CH)), tile, tile, tile, tile] + weight_specs,
        out_specs=flat,
        out_shape=shape((CELLS, CH), BF16),
        scratch_shapes=[
            pltpu.VMEM((4, 4, COLS, CH), BF16),
            pltpu.VMEM((3, 2, CELLS, HALF), F32),
        ],
        compiler_params=room(52),
        cost_estimate=estimate,
        name="conv",
    )(lat_flat, bias_row, act_late, earlier, act_low, act_high, kernel, kernel_other)

    part = pl.pallas_call(
        weight_kernel,
        out_shape=shape((384, 1152), F32),
        scratch_shapes=[
            pltpu.VMEM((3, 3, 1280, 128), BF16),
            pltpu.VMEM((8, 10, COLS, 128), BF16),
        ],
        compiler_params=room(24),
        cost_estimate=estimate,
        name="weight",
    )(mixed)
    keep, send = pl.pallas_call(
        border_kernel,
        out_shape=(shape((1736, 128), F32), shape((1736, 128), F32)),
        scratch_shapes=[
            pltpu.VMEM((1, 3, 1280, 128), BF16),
            pltpu.VMEM((4, 10, COLS, 128), BF16),
            pltpu.VMEM((384, 1152), F32),
        ],
        compiler_params=room(24),
        name="border",
    )(mixed, halo, part, sums)
    got = moved(send, "dp", 1)

    pieces = pl.pallas_call(
        split_kernel,
        out_shape=shape((8, 272, 128), BF16),
        scratch_shapes=[pltpu.VMEM((1736, 128), F32)],
        compiler_params=room(6),
        name="split",
    )(keep, got)
    pieces = lax.all_to_all(pieces, "z", 0, 0)
    spread = pl.pallas_call(
        sum_kernel,
        out_shape=shape((16, 72, 128), F32),
        scratch_shapes=[pltpu.VMEM((256, 128), F32)],
        compiler_params=room(4),
        name="sum",
    )(pieces)
    gathered = lax.all_to_all(spread, ("y", "x"), 0, 0)
    kernel_grad, gain_grad, bias_grad = pl.pallas_call(
        final_kernel,
        out_shape=(shape((432, 256), F32), shape((1, CH), F32), shape((1, CH), F32)),
        scratch_shapes=[pltpu.VMEM((512, 256), F32)],
        compiler_params=room(6),
        name="final",
    )(gathered)
    return (
        block_out.reshape(latents.shape),
        latent_grad.reshape(latents.shape),
        kernel_grad,
        gain_grad.reshape(CH),
        bias_grad.reshape(CH),
    )


def solution(mesh):
    fine = Mesh(mesh.devices.reshape(2, 8, 4, 4), ("dp", "z", "y", "x"))
    cells = P("dp", ("z", "y"), "x", None, None)
    return jax.shard_map(
        on_device,
        mesh=fine,
        in_specs=(cells, P(), P(None, "dp"), P(), cells),
        out_specs=(cells, cells, P(("z", "y"), "dp"), P(), P()),
        check_vma=False,
    )
```
